256 devices in a mesh: dom: 128 (over z, y, x), col: 2 (over core).
Axes of the slice: x: 4, y: 4, z: 8, core: 2. Of those that a mesh axis runs over, the one named last changes fastest.
Arguments:
- seed_data: bfloat16 [524288, 256], P('dom', 'col'), may hold values from -40 to 40
- dataset_order: int32 [128, 4096], P('dom'), may hold values from 0 to 4095, each once within a row
- affinity: bfloat16 [4096, 16, 128, 128], P('dom'), may hold values from 9.952637e-21 to 1
- neighbour_tiles: int32 [4096, 16], P('dom'), may hold values from 0 to 4095, as said below
- clamp_mask: int32 [524288], P('dom'), may hold values 0 or 1
Outputs:
- labels: bfloat16 [524288, 256], P('dom', 'col')
The draws below stay inside these ranges and needn't reach their ends.
Inputs may be any that keep to these rules, and one draw needn't show every extreme that they name: `neighbour_tiles`: slot 0 of row tile t is t itself. Every id names a tile of the row tile's own partition (id // 32) or of the partition just below or above it; partition 0 names none below and the last partition none above. Over all row tiles of one partition at most 4 distinct tiles of each neighbouring partition are named, and partition 0 names exactly 4 tiles of partition 1.
All inputs are finite; a program needn't handle non-finite values. No bound on the sum of `clamp_mask` on one device may be relied on, other than what follows from the above.
Results may differ from the reference program's by a relative error of at most 0.001.
Values may be sent and summed in bfloat16 or wider, within the bound.
No kernel may reach another device: no remote copies, remote signals or barrier semaphores. Data moves between devices by JAX's collectives and lax.ppermute only.
A program may use at most 128 MiB of HBM per device.

```python
import math
import jax
import jax.numpy as jnp
from jax import lax

TILE = 128
LABELS = 256
TILE_DEV = 32
SLOTS = 16
CAP = 4
ITERS = 3
NPART = 128
CELL_DEV = 4096
TILES = 4096
CELLS = 524288
N_DOM = 128


def draw_seed_data(key, part):
    keys = jax.random.split(key, 2)
    col_scale = 10.0 ** (jnp.arange(LABELS, dtype=jnp.float32) / (LABELS - 1) - 0.5)
    row_scale = 10.0 ** (jax.random.uniform(keys[0], (CELLS, 1), dtype=jnp.float32) - 0.5)
    base = jax.random.normal(keys[1], (CELLS, LABELS), dtype=jnp.float32)
    return jnp.clip(base * row_scale * col_scale[None, :], -40.0, 40.0).astype(jnp.bfloat16)


def draw_neighbour_tiles(key, part):
    keys = jax.random.split(key, 5)
    partition_index = jnp.arange(N_DOM, dtype=jnp.int32)
    left_count = jax.random.randint(keys[0], (N_DOM,), 1, CAP + 1).astype(jnp.int32)
    right_count = jax.random.randint(keys[1], (N_DOM,), 1, CAP + 1).astype(jnp.int32)
    right_count = jnp.where(partition_index == 0, CAP, right_count)
    left_count = jnp.where(partition_index == 0, 0, left_count)
    right_count = jnp.where(partition_index == N_DOM - 1, 0, right_count)
    left_pick = jax.vmap(lambda sub: jax.random.permutation(sub, TILE_DEV))(jax.random.split(keys[2], N_DOM)).astype(jnp.int32)
    right_pick = jax.vmap(lambda sub: jax.random.permutation(sub, TILE_DEV))(jax.random.split(keys[3], N_DOM)).astype(jnp.int32)
    width = TILE_DEV + 2 * CAP
    slot_ids = jnp.broadcast_to(jnp.arange(width, dtype=jnp.int32)[None, :], (N_DOM, width))
    own_ids = partition_index[:, None] * TILE_DEV + jnp.clip(slot_ids, 0, TILE_DEV - 1)
    left_pos = jnp.clip(slot_ids - TILE_DEV, 0, TILE_DEV - 1)
    left_ids = (partition_index[:, None] - 1) * TILE_DEV + jnp.take_along_axis(left_pick, left_pos, axis=1)
    right_pos = jnp.clip(slot_ids - TILE_DEV - left_count[:, None], 0, TILE_DEV - 1)
    right_ids = (partition_index[:, None] + 1) * TILE_DEV + jnp.take_along_axis(right_pick, right_pos, axis=1)
    pool_ids = jnp.where(slot_ids < TILE_DEV, own_ids, jnp.where(slot_ids < TILE_DEV + left_count[:, None], left_ids, right_ids))
    pool_size = TILE_DEV + left_count + right_count
    picks = jax.random.randint(keys[4], (N_DOM, TILE_DEV, SLOTS), 0, pool_size[:, None, None]).astype(jnp.int32)
    row_ids = jnp.broadcast_to(jnp.arange(TILE_DEV, dtype=jnp.int32)[None, :], (N_DOM, TILE_DEV))
    slot_zero = row_ids
    slot_one = jnp.where(row_ids < left_count[:, None], TILE_DEV + row_ids, picks[:, :, 1])
    slot_two = jnp.where(row_ids < right_count[:, None], TILE_DEV + left_count[:, None] + row_ids, picks[:, :, 2])
    chosen = jnp.concatenate([slot_zero[:, :, None], slot_one[:, :, None], slot_two[:, :, None], picks[:, :, 3:]], axis=2)
    full_pool_rows = jnp.broadcast_to(pool_ids[:, None, :], (N_DOM, TILE_DEV, width))
    result = jnp.take_along_axis(full_pool_rows, chosen, axis=2)
    return result.reshape(N_DOM * TILE_DEV, SLOTS).astype(jnp.int32)


def plant(values, stream_key, smallest, top_value):
    longest = values.shape.index(max(values.shape))
    spots = []
    for shift in (0, 1):
        where = [jax.random.randint(jax.random.fold_in(stream_key, axis), (), 0, length) for axis, length in enumerate(values.shape)]
        where[longest] = (where[longest] + shift) % values.shape[longest]
        spots.append(tuple(where))
    return values.at[spots[0]].set(smallest).at[spots[1]].set(top_value)


def block_levels(stream_key, dims, pieces, least, top_value):
    level, own = 1.0, jax.random.fold_in(stream_key, 6)
    for position, shards_of in pieces:
        steps = jnp.exp(jax.random.uniform(jax.random.fold_in(own, position), (shards_of,), jnp.float32, least / len(pieces), top_value / len(pieces)))
        level = level * jnp.repeat(steps, dims[position] // shards_of).reshape([-1 if axis == position else 1 for axis in range(len(dims))])
    return level


def setup_inputs(seed: int = 0) -> dict:
    streams_of = jax.random.split(jax.random.key(seed), 6)
    return {
        "seed_data": draw_seed_data(jax.random.fold_in(streams_of[5], 71), 0),
        "dataset_order": jax.vmap(lambda own: jax.random.permutation(own, CELL_DEV))(jax.random.split(streams_of[1], NPART)).reshape((NPART, CELL_DEV)).astype(jnp.int32),
        "affinity": jnp.clip(jnp.exp(math.log(1.0) - 46.05645 * jax.random.uniform(streams_of[2], (TILES, SLOTS, TILE, TILE), jnp.float32) ** block_levels(streams_of[2], (TILES, SLOTS, TILE, TILE), ((0, 128),), -0.2, 0.2)), 9.952637130238029e-21, 1.0).astype(jnp.bfloat16),
        "neighbour_tiles": draw_neighbour_tiles(jax.random.fold_in(streams_of[5], 71), 0),
        "clamp_mask": plant((jax.random.randint(streams_of[4], (CELLS,), 0, 5) < 4).astype(jnp.int32), jax.random.fold_in(streams_of[4], 1), 0, 1),
    }


carry_weight = 0.9
norm_eps = 1e-05

def reference(seed_data, dataset_order, affinity, neighbour_tiles, clamp_mask):
    per_source = CELL_DEV // N_DOM
    partition_index = jnp.arange(N_DOM, dtype=jnp.int32)[:, None]
    sender_partition = dataset_order // per_source * CELL_DEV + partition_index * per_source + dataset_order % per_source
    clamped_label_rows = seed_data[sender_partition.reshape(-1).astype(jnp.int32)]
    seed_float = clamped_label_rows.astype(jnp.float32)
    tile_blocks = affinity.reshape(N_DOM, TILE_DEV, SLOTS, TILE, TILE)
    ref_blocks = neighbour_tiles.reshape(N_DOM, TILE_DEV, SLOTS)
    degree = lax.map(lambda edge_weight_values: lax.optimization_barrier(jnp.sum(edge_weight_values.astype(jnp.float32), axis=(1, 3))), tile_blocks)
    degree = degree.reshape(CELLS, 1)
    labels = clamped_label_rows
    for iteration in range(ITERS):
        current = labels.reshape(TILES, TILE, LABELS)

        def spread_block(block_args):
            edge_weight_values, tile_refs = block_args
            gathered_rows = current[tile_refs].astype(jnp.float32)
            return jnp.einsum('xzeh,xzhj->xej', edge_weight_values.astype(jnp.float32), gathered_rows)
        diffused_labels = lax.map(spread_block, (tile_blocks, ref_blocks)).reshape(CELLS, LABELS)
        mixed = carry_weight * diffused_labels / degree + (1.0 - carry_weight) * seed_float
        row_scale = jnp.sqrt(lax.optimization_barrier(jnp.mean(mixed * mixed, axis=1)) + norm_eps)
        labels = jnp.where(clamp_mask[:, None] == 1, seed_float, mixed / row_scale[:, None]).astype(jnp.bfloat16)
    return labels
```

```python
import functools

import jax
import jax.numpy as jnp
from jax import lax
from jax.experimental import pallas as pl
from jax.experimental.pallas import tpu as pltpu
from jax.sharding import PartitionSpec as P


ITERS = 3
TILE = 128
TILES = 32
SLOTS = 16
CAP = 4
LATE = 6
EARLY = SLOTS - LATE
ZERO = TILES
COLS = 256

carry_weight = 0.9
norm_eps = 1e-05

VMEM = pl.BlockSpec(memory_space=pltpu.VMEM)
SMEM = pl.BlockSpec(memory_space=pltpu.SMEM)
MIB = 1 << 20


def in_vmem(shape, dtype):
    return pltpu.VMEM(shape, dtype)


def tables_kernel(nt_ref, tile_ref, slot_ref, rest_ref, below_ref, above_ref, place_ref):
    base = nt_ref[0] - TILES

    def clear(j, c):
        place_ref[j] = 0
        return c

    lax.fori_loop(0, 3 * TILES, clear, 0)

    def mark(e, c):
        place_ref[nt_ref[e] - base] = 1
        return c

    lax.fori_loop(0, TILES * SLOTS, mark, 0, unroll=8)
    for q in range(128):
        below_ref[q] = 0
        above_ref[q] = 0

    def name(j, c):
        count_below, count_above = c
        far = j + 2 * TILES
        is_below = place_ref[j]
        is_above = place_ref[far]

        @pl.when(is_below == 1)
        def _():
            below_ref[jnp.minimum(count_below, CAP - 1)] = j

        @pl.when(is_above == 1)
        def _():
            above_ref[jnp.minimum(count_above, CAP - 1)] = j

        place_ref[j] = ZERO + 1 + count_below
        place_ref[far] = ZERO + 1 + CAP + count_above
        place_ref[j + TILES] = j
        return count_below + is_below, count_above + is_above

    lax.fori_loop(0, TILES, name, (0, 0))

    def row(t, total):
        head, tail = t * SLOTS, t * SLOTS + SLOTS - 1
        for k in range(SLOTS):
            off = nt_ref[t * SLOTS + k] - base
            own = ((off >= TILES) & (off < 2 * TILES)).astype(jnp.int32)
            at = jnp.where(own == 1, head, tail)
            tile_ref[at] = place_ref[off]
            slot_ref[at] = t * SLOTS + k
            head = head + own
            tail = tail - (1 - own)
        rest = jnp.maximum(EARLY - (head - t * SLOTS), 0)
        rest_ref[t] = rest
        return total + rest

    rest_ref[TILES] = lax.fori_loop(0, TILES, row, 0)


def tables(nt):
    n = TILES * SLOTS
    i32 = lambda k: jax.ShapeDtypeStruct((k,), jnp.int32)
    return pl.pallas_call(
        tables_kernel,
        out_shape=(i32(n), i32(n), i32(128), i32(128), i32(128)),
        in_specs=[SMEM],
        out_specs=(SMEM,) * 5,
        scratch_shapes=[pltpu.SMEM((3 * TILES,), jnp.int32)],
        compiler_params=pltpu.CompilerParams(vmem_limit_bytes=MIB),
        cost_estimate=pl.CostEstimate(flops=0, bytes_accessed=16 * MIB, transcendentals=0),
        name="tables",
    )(nt)


def stage_kernel(a_ref, clamp_ref, inv_ref, held_ref, v_ref, sem):
    step = 4
    copies = [
        pltpu.make_async_copy(a_ref.at[pl.ds(g * step, step)], v_ref.at[pl.ds(g * step, step)], sem.at[g])
        for g in range(TILES // step)
    ]
    for c in copies:
        c.start()
    lane = lax.broadcasted_iota(jnp.int32, (TILE, TILE), 1)
    inv_ref[...] = jnp.zeros((TILE, TILE), jnp.float32)
    clamp = clamp_ref[...].astype(jnp.float32)
    held_ref[...] = jnp.concatenate([clamp, jnp.zeros((TILE - TILES, TILE), jnp.float32)], axis=0).T
    for g, c in enumerate(copies):
        c.wait()

        def body(u, carry, g=g):
            t = g * step + u
            total = jnp.zeros((TILE, TILE), jnp.float32)
            for k in range(SLOTS):
                total = total + v_ref[t, k].astype(jnp.float32)
            inv = carry_weight / jnp.sum(total, axis=1, keepdims=True)
            inv_ref[...] = jnp.where(lane == t, inv, inv_ref[...])
            return carry

        lax.fori_loop(0, step, body, 0)


def stage(affinity, clamp):
    return pl.pallas_call(
        stage_kernel,
        out_shape=(
            jax.ShapeDtypeStruct((TILE, TILE), jnp.float32),
            jax.ShapeDtypeStruct((TILE, TILE), jnp.float32),
        ),
        in_specs=[pl.BlockSpec(memory_space=pltpu.HBM), VMEM],
        out_specs=(VMEM,) * 2,
        scratch_shapes=[pltpu.VMEM(affinity.shape, jnp.bfloat16), pltpu.SemaphoreType.DMA((TILES // 4,))],
        compiler_params=pltpu.CompilerParams(vmem_limit_bytes=42 * MIB),
        cost_estimate=pl.CostEstimate(flops=TILES * SLOTS * TILE * TILE, bytes_accessed=16 * MIB, transcendentals=0),
        name="stage",
    )(affinity, clamp)


def both_kernel(to_below, to_above, asked):
    for r in range(CAP):
        asked[r] = to_below[r]
        asked[CAP + r] = to_above[r]


def both(to_below, to_above):
    return pl.pallas_call(
        both_kernel,
        out_shape=jax.ShapeDtypeStruct((128,), jnp.int32),
        in_specs=[SMEM] * 2,
        out_specs=SMEM,
        compiler_params=pltpu.CompilerParams(vmem_limit_bytes=MIB),
        name="both",
    )(to_below, to_above)


def pack_sends(send_below_ref, send_above_ref, pool_ref, asked):
    for r in range(CAP):
        send_below_ref[r] = pool_ref[asked[r]]
        send_above_ref[r] = pool_ref[asked[CAP + r]]


def order_kernel(order_ref, asked, own_ref, other_ref, a_ref, pool_ref, send_below_ref, send_above_ref, v_ref, src, dst, sem):
    load = pltpu.make_async_copy(a_ref, v_ref, sem)
    load.start()
    src[:, 0:TILE] = own_ref[...].astype(jnp.float32)
    src[:, TILE:COLS] = other_ref[...].astype(jnp.float32)
    unroll = 32

    def step(i, c):
        base = pl.multiple_of(i * unroll, unroll)
        for u in range(unroll):
            dst[pl.ds(base + u, 1), :] = src[pl.ds(order_ref[base + u], 1), :]
        return c

    lax.fori_loop(0, TILES * TILE // unroll, step, 0)
    pool_ref[0:TILES] = dst[...].astype(jnp.bfloat16).reshape(TILES, TILE, COLS)
    pool_ref[ZERO] = jnp.zeros((TILE, COLS), jnp.bfloat16)
    pack_sends(send_below_ref, send_above_ref, pool_ref, asked)
    load.wait()


POOL = (TILES + 1, TILE, COLS)
SEND = (CAP, TILE, COLS)


def order_rows(order, asked, own, other, affinity):
    return pl.pallas_call(
        order_kernel,
        out_shape=(
            in_vmem(POOL, jnp.bfloat16),
            in_vmem(SEND, jnp.bfloat16),
            in_vmem(SEND, jnp.bfloat16),
            in_vmem(affinity.shape, jnp.bfloat16),
        ),
        in_specs=[SMEM, SMEM, VMEM, VMEM, pl.BlockSpec(memory_space=pltpu.HBM)],
        out_specs=(VMEM,) * 4,
        scratch_shapes=[pltpu.VMEM((TILES * TILE, COLS), jnp.float32)] * 2 + [pltpu.SemaphoreType.DMA],
        compiler_params=pltpu.CompilerParams(vmem_limit_bytes=32 * MIB),
        name="order_rows",
    )(order, asked, own, other, affinity)


def early_kernel(tile_ref, slot_ref, a_ref, pool_ref, acc_ref):
    unroll = 4

    def step(g, c):
        for u in range(unroll):
            t = g * unroll + u
            lhs, rhs = [], []
            for k in range(EARLY):
                tile = tile_ref[t * SLOTS + k]
                lhs.append(a_ref[slot_ref[t * SLOTS + k]])
                rhs.append(pool_ref[jnp.minimum(tile, ZERO)])
            acc_ref[t] = jnp.dot(
                jnp.concatenate(lhs, axis=1), jnp.concatenate(rhs, axis=0), preferred_element_type=jnp.float32
            )
        return c

    lax.fori_loop(0, TILES // unroll, step, 0)


def early(tile, slot, a, pool):
    flops = 2 * TILES * EARLY * TILE * TILE * COLS
    return pl.pallas_call(
        early_kernel,
        out_shape=in_vmem((TILES, TILE, COLS), jnp.float32),
        in_specs=[SMEM, SMEM, VMEM, VMEM],
        out_specs=VMEM,
        compiler_params=pltpu.CompilerParams(vmem_limit_bytes=8 * MIB),
        cost_estimate=pl.CostEstimate(flops=flops, bytes_accessed=16 * MIB, transcendentals=0),
        name="early",
    )(tile, slot, a, pool)


def late_kernel(last, tile_ref, slot_ref, rest_ref, asked, a_ref, acc_in, pool_ref, below_ref, above_ref,
                seed_ref, inv_ref, clamp_ref, acc_ref, *refs):
    if last:
        out_ref, every = refs
    else:
        new_ref, send_below_ref, send_above_ref, every = refs
    every[0 : TILES + 1] = pool_ref[...]
    every[TILES + 1 : TILES + 1 + CAP] = below_ref[...]
    every[TILES + 1 + CAP :] = above_ref[...]

    @pl.when(rest_ref[TILES] > 0)
    def _():
        def row(t, c):
            def one(r, c):
                at = t * SLOTS + EARLY - 1 - r
                acc_ref[t] = acc_ref[t] + jnp.dot(
                    a_ref[slot_ref[at]], every[tile_ref[at]], preferred_element_type=jnp.float32
                )
                return c

            return lax.fori_loop(0, rest_ref[t], one, c)

        lax.fori_loop(0, TILES, row, 0)

    unroll = 4
    lane = lax.broadcasted_iota(jnp.int32, (TILE, TILE), 1)

    def step(g, c):
        for u in range(unroll):
            t = g * unroll + u
            lhs, rhs = [], []
            for k in range(EARLY, SLOTS):
                lhs.append(a_ref[slot_ref[t * SLOTS + k]])
                rhs.append(every[tile_ref[t * SLOTS + k]])
            spread = acc_ref[t] + jnp.dot(
                jnp.concatenate(lhs, axis=1), jnp.concatenate(rhs, axis=0), preferred_element_type=jnp.float32
            )
            mine = lane == t
            inv = jnp.sum(jnp.where(mine, inv_ref[...], 0.0), axis=1, keepdims=True)
            held = jnp.sum(jnp.where(mine, clamp_ref[...], 0.0), axis=1, keepdims=True)
            seed = seed_ref[t].astype(jnp.float32)
            mixed = spread * inv + (1.0 - carry_weight) * seed
            mean = jnp.sum(mixed * mixed, axis=1, keepdims=True) * (1.0 / COLS)
            scaled = mixed * lax.rsqrt(mean + norm_eps)
            new = jnp.where(held > 0.5, seed, scaled).astype(jnp.bfloat16)
            if last:
                out_ref[t] = new[:, 0:TILE]
            else:
                new_ref[t] = new
        return c

    lax.fori_loop(0, TILES // unroll, step, 0)
    if not last:
        new_ref[ZERO] = jnp.zeros((TILE, COLS), jnp.bfloat16)
        pack_sends(send_below_ref, send_above_ref, new_ref, asked)


def late(last, tile, slot, rest, asked, a, acc, pool, below, above, seed, inv, clamp):
    acc_out = in_vmem((TILES, TILE, COLS), jnp.float32)
    if last:
        outs = (acc_out, jax.ShapeDtypeStruct((TILES, TILE, TILE), jnp.bfloat16))
    else:
        outs = (acc_out, in_vmem(POOL, jnp.bfloat16), in_vmem(SEND, jnp.bfloat16), in_vmem(SEND, jnp.bfloat16))
    return pl.pallas_call(
        functools.partial(late_kernel, last),
        out_shape=outs,
        in_specs=[SMEM] * 4 + [VMEM] * 8,
        out_specs=(VMEM,) * len(outs),
        input_output_aliases={5: 0},
        scratch_shapes=[pltpu.VMEM((TILES + 1 + 2 * CAP, TILE, COLS), jnp.bfloat16)],
        compiler_params=pltpu.CompilerParams(vmem_limit_bytes=8 * MIB),
        name="late_last" if last else "late",
    )(tile, slot, rest, asked, a, acc, pool, below, above, seed, inv, clamp)[1:]


def shifted(block, distance):
    devices = range(lax.axis_size("dom"))
    route = [(i - distance, i) for i in devices if i - distance in devices]
    return lax.ppermute(block, "dom", route)


def per_device(seed_data, dataset_order, affinity, neighbour_tiles, clamp_mask):
    part_count = lax.axis_size("dom")
    cell_count, slab = seed_data.shape
    pieces = seed_data.reshape(part_count, cell_count // part_count, slab)
    own = lax.all_to_all(pieces, "dom", split_axis=0, concat_axis=0, tiled=True).reshape(cell_count, slab)
    tile, slot, rest, need_below, need_above = tables(neighbour_tiles.reshape(-1))
    to_above = shifted(need_below, -1)
    to_below = shifted(need_above, 1)
    asked = both(to_below, to_above)
    inv, clamp = stage(affinity, clamp_mask.reshape(TILES, TILE))
    other = lax.ppermute(own, "col", [(0, 1), (1, 0)])
    affinity = affinity.reshape(TILES * SLOTS, TILE, TILE)
    pool, send_below, send_above, a = order_rows(dataset_order.reshape(-1), asked, own, other, affinity)
    seed = pool
    for iteration in range(ITERS):
        above = shifted(send_below, -1)
        below = shifted(send_above, 1)
        acc = early(tile, slot, a, pool)
        last = iteration == ITERS - 1
        result = late(last, tile, slot, rest, asked, a, acc, pool, below, above, seed, inv, clamp)
        if last:
            return result[0].reshape(cell_count, slab)
        pool, send_below, send_above = result


def solution(mesh):
    return jax.shard_map(
        per_device,
        mesh=mesh,
        in_specs=(
            P("dom", "col"),
            P("dom", None),
            P("dom", None, None, None),
            P("dom", None),
            P("dom"),
        ),
        out_specs=P("dom", "col"),
        check_vma=False,
    )
```

```python
import jax
import jax.numpy as jnp
from jax import lax
from jax.experimental import pallas as pl
from jax.experimental.pallas import tpu as pltpu
from jax.sharding import PartitionSpec as P


ITERS = 3
TILE = 128
TILES = 32
SLOTS = 16
SLOT_AT = TILES * SLOTS
CAP = 4
EARLY = 10
REST_AT = 2 * TILES * SLOTS
ZERO = TILES
COLS = 256

carry_weight = 0.9
norm_eps = 1e-05

VMEM = pl.BlockSpec(memory_space=pltpu.VMEM)
SMEM = pl.BlockSpec(memory_space=pltpu.SMEM)
MIB = 1 << 20


def in_vmem(shape, dtype):
    return pltpu.VMEM(shape, dtype)


def tables_kernel(nt_ref, core_ref, table_ref, need_ref, place_ref):
    base = nt_ref[0] - TILES
    direct = jnp.where(core_ref[0] == 0, 2 * TILES, 0)
    swapped = 2 * TILES - direct

    def clear(j, c):
        place_ref[j] = 0
        return c

    lax.fori_loop(0, 3 * TILES, clear, 0)

    def mark(e, c):
        place_ref[nt_ref[e] - base] = 1
        return c

    lax.fori_loop(0, TILES * SLOTS, mark, 0, unroll=8)
    for q in range(128):
        need_ref[q] = 0

    def name(j, c):
        count_direct, count_swapped = c
        is_direct = place_ref[direct + j]
        is_swapped = place_ref[swapped + j]

        @pl.when(is_direct == 1)
        def _():
            need_ref[jnp.minimum(count_direct, CAP - 1)] = j

        place_ref[direct + j] = ZERO + 1 + count_direct
        place_ref[swapped + j] = ZERO + 1 + CAP + count_swapped
        place_ref[j + TILES] = j
        return count_direct + is_direct, count_swapped + is_swapped

    lax.fori_loop(0, TILES, name, (0, 0))

    def row(t, total):
        head, tail = t * SLOTS, t * SLOTS + SLOTS - 1
        for k in range(SLOTS):
            off = nt_ref[t * SLOTS + k] - base
            own = ((off >= TILES) & (off < 2 * TILES)).astype(jnp.int32)
            at = jnp.where(own == 1, head, tail)
            table_ref[at] = place_ref[off]
            table_ref[SLOT_AT + at] = t * SLOTS + k
            head = head + own
            tail = tail - (1 - own)
        rest = jnp.maximum(EARLY - (head - t * SLOTS), 0)
        table_ref[REST_AT + t] = rest
        return total + rest

    table_ref[REST_AT + TILES] = lax.fori_loop(0, TILES, row, 0)


def tables(nt, core):
    i32 = lambda k: jax.ShapeDtypeStruct((k,), jnp.int32)
    return pl.pallas_call(
        tables_kernel,
        out_shape=(i32(REST_AT + 128), i32(128)),
        in_specs=[SMEM] * 2,
        out_specs=(SMEM,) * 2,
        scratch_shapes=[pltpu.SMEM((3 * TILES,), jnp.int32)],
        compiler_params=pltpu.CompilerParams(vmem_limit_bytes=MIB),
        cost_estimate=pl.CostEstimate(flops=0, bytes_accessed=16 * MIB, transcendentals=0),
        name="tables",
    )(nt, core)


def stage_kernel(a_ref, clamp_ref, inv_ref, held_ref, v_ref, sem):
    step = 4
    copies = [
        pltpu.make_async_copy(a_ref.at[pl.ds(g * step, step)], v_ref.at[pl.ds(g * step, step)], sem.at[g])
        for g in range(TILES // step)
    ]
    for c in copies:
        c.start()
    lane = lax.broadcasted_iota(jnp.int32, (TILE, TILE), 1)
    inv_ref[...] = jnp.zeros((TILE, TILE), jnp.float32)
    clamp = clamp_ref[...].astype(jnp.float32)
    held_ref[...] = jnp.concatenate([clamp, jnp.zeros((TILE - TILES, TILE), jnp.float32)], axis=0).T
    for g, c in enumerate(copies):
        c.wait()

        def body(u, carry, g=g):
            t = g * step + u
            total = jnp.zeros((TILE, TILE), jnp.float32)
            for k in range(SLOTS):
                total = total + v_ref[t, k].astype(jnp.float32)
            inv = carry_weight / jnp.sum(total, axis=1, keepdims=True)
            inv_ref[...] = jnp.where(lane == t, inv, inv_ref[...])
            return carry

        lax.fori_loop(0, step, body, 0)


def stage(affinity, clamp):
    return pl.pallas_call(
        stage_kernel,
        out_shape=(
            jax.ShapeDtypeStruct((TILE, TILE), jnp.float32),
            jax.ShapeDtypeStruct((TILE, TILE), jnp.float32),
        ),
        in_specs=[pl.BlockSpec(memory_space=pltpu.HBM), VMEM],
        out_specs=(VMEM,) * 2,
        scratch_shapes=[pltpu.VMEM(affinity.shape, jnp.bfloat16), pltpu.SemaphoreType.DMA((TILES // 4,))],
        compiler_params=pltpu.CompilerParams(vmem_limit_bytes=42 * MIB),
        cost_estimate=pl.CostEstimate(flops=TILES * SLOTS * TILE * TILE, bytes_accessed=16 * MIB, transcendentals=0),
        name="stage",
    )(affinity, clamp)


POOL = (TILES + 1, TILE, COLS)
HALF = (TILES + 1, TILE, TILE)
SEND = (CAP, TILE, COLS)


def order_kernel(order_ref, own_ref, a_ref, half_ref, v_ref, src, dst, sem):
    load = pltpu.make_async_copy(a_ref, v_ref, sem)
    load.start()
    src[...] = own_ref[...].astype(jnp.float32)
    unroll = 64

    def step(i, c):
        base = pl.multiple_of(i * unroll, unroll)
        for u in range(unroll):
            dst[pl.ds(base + u, 1), :] = src[pl.ds(order_ref[base + u], 1), :]
        return c

    lax.fori_loop(0, TILES * TILE // unroll, step, 0)
    half_ref[0:TILES] = dst[...].astype(jnp.bfloat16).reshape(TILES, TILE, TILE)
    half_ref[ZERO] = jnp.zeros((TILE, TILE), jnp.bfloat16)
    load.wait()


def order_rows(order, own, affinity):
    return pl.pallas_call(
        order_kernel,
        out_shape=(in_vmem(HALF, jnp.bfloat16), in_vmem(affinity.shape, jnp.bfloat16)),
        in_specs=[SMEM, VMEM, pl.BlockSpec(memory_space=pltpu.HBM)],
        out_specs=(VMEM,) * 2,
        scratch_shapes=[pltpu.VMEM((TILES * TILE, TILE), jnp.float32)] * 2 + [pltpu.SemaphoreType.DMA],
        compiler_params=pltpu.CompilerParams(vmem_limit_bytes=32 * MIB),
        name="order_rows",
    )(order, own, affinity)


def labels_of(refs, tile):
    parts = [ref[tile] for ref in refs]
    return parts[0] if len(parts) == 1 else jnp.concatenate(parts, axis=1)


def pack_kernel(asked, *refs):
    for r in range(CAP):
        refs[-1][r] = labels_of(refs[:-1], asked[r])


def pack(asked, labels):
    return pl.pallas_call(
        pack_kernel,
        out_shape=in_vmem(SEND, jnp.bfloat16),
        in_specs=[SMEM] + [VMEM] * len(labels),
        out_specs=VMEM,
        compiler_params=pltpu.CompilerParams(vmem_limit_bytes=MIB),
        name="pack",
    )(asked, *labels)


def early_kernel(table, a_ref, *refs):
    acc_ref, labels = refs[-1], refs[:-1]
    unroll = 4

    def step(g, c):
        for u in range(unroll):
            t = g * unroll + u
            lhs, rhs = [], []
            for k in range(EARLY):
                lhs.append(a_ref[table[SLOT_AT + t * SLOTS + k]])
                rhs.append(labels_of(labels, jnp.minimum(table[t * SLOTS + k], ZERO)))
            acc_ref[t] = jnp.dot(
                jnp.concatenate(lhs, axis=1), jnp.concatenate(rhs, axis=0), preferred_element_type=jnp.float32
            )
        return c

    lax.fori_loop(0, TILES // unroll, step, 0)


def early(table, a, labels):
    flops = 2 * TILES * EARLY * TILE * TILE * COLS
    return pl.pallas_call(
        early_kernel,
        out_shape=in_vmem((TILES, TILE, COLS), jnp.float32),
        in_specs=[SMEM] + [VMEM] * (1 + len(labels)),
        out_specs=VMEM,
        compiler_params=pltpu.CompilerParams(vmem_limit_bytes=8 * MIB),
        cost_estimate=pl.CostEstimate(flops=flops, bytes_accessed=16 * MIB, transcendentals=0),
        name="early",
    )(table, a, *labels)


def gather_pool(every, labels, direct_ref, swapped_ref):
    width = COLS // len(labels)
    for p, ref in enumerate(labels):
        every[0 : TILES + 1, :, p * width : (p + 1) * width] = ref[...]
    every[TILES + 1 : TILES + 1 + CAP] = direct_ref[...]
    every[TILES + 1 + CAP :, :, :TILE] = swapped_ref[:, :, TILE:]
    every[TILES + 1 + CAP :, :, TILE:] = swapped_ref[:, :, :TILE]


def add_rest(table, a_ref, every, acc_ref):
    @pl.when(table[REST_AT + TILES] > 0)
    def _():
        def row(t, c):
            def one(r, c):
                at = t * SLOTS + EARLY - 1 - r
                acc_ref[t] = acc_ref[t] + jnp.dot(
                    a_ref[table[SLOT_AT + at]], every[table[at]], preferred_element_type=jnp.float32
                )
                return c

            return lax.fori_loop(0, table[REST_AT + t], one, c)

        lax.fori_loop(0, TILES, row, 0)


def new_labels(table, a_ref, every, acc_ref, inv_ref, held_ref, seeds, t, width):
    lhs, rhs = [], []
    for k in range(EARLY, SLOTS):
        lhs.append(a_ref[table[SLOT_AT + t * SLOTS + k]])
        rhs.append(every[table[t * SLOTS + k]])
    spread = acc_ref[t] + jnp.dot(
        jnp.concatenate(lhs, axis=1), jnp.concatenate(rhs, axis=0), preferred_element_type=jnp.float32
    )
    mine = lax.broadcasted_iota(jnp.int32, (TILE, TILE), 1) == t
    inv = jnp.sum(jnp.where(mine, inv_ref[...], 0.0), axis=1, keepdims=True)
    held = jnp.sum(jnp.where(mine, held_ref[...], 0.0), axis=1, keepdims=True)
    seed = jnp.concatenate([ref[t] for ref in seeds], axis=1).astype(jnp.float32)
    mixed = spread * inv + (1.0 - carry_weight) * seed
    square = mixed * mixed
    mean = jnp.sum(square[:, :TILE] + square[:, TILE:], axis=1, keepdims=True) * (1.0 / COLS)
    scaled = mixed[:, :width] * lax.rsqrt(mean + norm_eps)
    return jnp.where(held > 0.5, seed[:, :width], scaled).astype(jnp.bfloat16)


def asked_kernel(table, asked, a_ref, acc_in, direct_ref, swapped_ref, inv_ref, held_ref, *refs):
    labels, seeds, (acc_ref, every, send_ref) = refs[:-5], refs[-5:-3], refs[-3:]
    gather_pool(every, labels, direct_ref, swapped_ref)
    add_rest(table, a_ref, every, acc_ref)
    for r in range(CAP):
        send_ref[r] = new_labels(table, a_ref, every, acc_ref, inv_ref, held_ref, seeds, asked[r], COLS)


def asked_tiles(table, asked, a, acc, direct, swapped, inv, held, labels, seeds):
    return pl.pallas_call(
        asked_kernel,
        out_shape=(
            in_vmem((TILES, TILE, COLS), jnp.float32),
            in_vmem(EVERY, jnp.bfloat16),
            in_vmem(SEND, jnp.bfloat16),
        ),
        in_specs=[SMEM] * 2 + [VMEM] * (6 + len(labels) + len(seeds)),
        out_specs=(VMEM,) * 3,
        input_output_aliases={3: 0},
        compiler_params=pltpu.CompilerParams(vmem_limit_bytes=4 * MIB),
        name="asked_tiles",
    )(table, asked, a, acc, direct, swapped, inv, held, *labels, *seeds)


EVERY = (TILES + 1 + 2 * CAP, TILE, COLS)


def all_kernel(table, a_ref, acc_ref, every, inv_ref, held_ref, *refs):
    seeds, new_ref = refs[:-1], refs[-1]
    unroll = 4

    def step(g, c):
        for u in range(unroll):
            t = g * unroll + u
            new_ref[t] = new_labels(table, a_ref, every, acc_ref, inv_ref, held_ref, seeds, t, COLS)
        return c

    lax.fori_loop(0, TILES // unroll, step, 0)
    new_ref[ZERO] = jnp.zeros((TILE, COLS), jnp.bfloat16)


def all_tiles(table, a, acc, every, inv, held, seeds):
    flops = 2 * TILES * (SLOTS - EARLY) * TILE * TILE * COLS
    return pl.pallas_call(
        all_kernel,
        out_shape=in_vmem(POOL, jnp.bfloat16),
        in_specs=[SMEM] + [VMEM] * (5 + len(seeds)),
        out_specs=VMEM,
        compiler_params=pltpu.CompilerParams(vmem_limit_bytes=8 * MIB),
        cost_estimate=pl.CostEstimate(flops=flops, bytes_accessed=16 * MIB, transcendentals=0),
        name="all_tiles",
    )(table, a, acc, every, inv, held, *seeds)


def last_kernel(table, a_ref, acc_in, direct_ref, swapped_ref, inv_ref, held_ref, *refs):
    labels, seeds, (acc_ref, out_ref, every) = refs[:-5], refs[-5:-3], refs[-3:]
    gather_pool(every, labels, direct_ref, swapped_ref)
    add_rest(table, a_ref, every, acc_ref)
    unroll = 4

    def step(g, c):
        for u in range(unroll):
            t = g * unroll + u
            out_ref[t] = new_labels(table, a_ref, every, acc_ref, inv_ref, held_ref, seeds, t, TILE)
        return c

    lax.fori_loop(0, TILES // unroll, step, 0)


def last_tiles(table, a, acc, direct, swapped, inv, held, labels, seeds):
    return pl.pallas_call(
        last_kernel,
        out_shape=(
            in_vmem((TILES, TILE, COLS), jnp.float32),
            jax.ShapeDtypeStruct((TILES, TILE, TILE), jnp.bfloat16),
        ),
        in_specs=[SMEM] + [VMEM] * (6 + len(labels) + len(seeds)),
        out_specs=(VMEM,) * 2,
        input_output_aliases={2: 0},
        scratch_shapes=[pltpu.VMEM(EVERY, jnp.bfloat16)],
        compiler_params=pltpu.CompilerParams(vmem_limit_bytes=8 * MIB),
        name="last_tiles",
    )(table, a, acc, direct, swapped, inv, held, *labels, *seeds)[1]


def shifted(block, step):
    parts, cores = lax.axis_size("dom"), lax.axis_size("col")
    route = []
    for i in range(parts):
        for core, to in ((0, i + step), (1, i - step)):
            if 0 <= to < parts:
                route.append((i * cores + core, to * cores + core))
    return lax.ppermute(block, ("dom", "col"), route)


def swapped_cores(block):
    return lax.ppermute(block, "col", [(0, 1), (1, 0)])


def per_device(seed_data, dataset_order, affinity, neighbour_tiles, clamp_mask):
    part_count = lax.axis_size("dom")
    cell_count, slab = seed_data.shape
    pieces = seed_data.reshape(part_count, cell_count // part_count, slab)
    own = lax.all_to_all(pieces, "dom", split_axis=0, concat_axis=0, tiled=True).reshape(cell_count, slab)
    core = lax.axis_index("col").astype(jnp.int32).reshape(1)
    table, need = tables(neighbour_tiles.reshape(-1), core)
    asked = shifted(need, 1)
    inv, held = stage(affinity, clamp_mask.reshape(TILES, TILE))
    affinity = affinity.reshape(TILES * SLOTS, TILE, TILE)
    half, a = order_rows(dataset_order.reshape(-1), own, affinity)
    labels = (half, swapped_cores(half))
    seeds = labels
    send = pack(asked, labels)
    for iteration in range(ITERS):
        direct = shifted(send, -1)
        if iteration > 0:
            labels = (all_tiles(table, a, acc, every, inv, held, seeds),)
        acc = early(table, a, labels)
        swapped = swapped_cores(direct)
        if iteration == ITERS - 1:
            result = last_tiles(table, a, acc, direct, swapped, inv, held, labels, seeds)
            return result.reshape(cell_count, slab)
        acc, every, send = asked_tiles(table, asked, a, acc, direct, swapped, inv, held, labels, seeds)


def solution(mesh):
    return jax.shard_map(
        per_device,
        mesh=mesh,
        in_specs=(
            P("dom", "col"),
            P("dom", None),
            P("dom", None, None, None),
            P("dom", None),
            P("dom"),
        ),
        out_specs=P("dom", "col"),
        check_vma=False,
    )
```

```python
import functools

import jax
import jax.numpy as jnp
from jax import lax
from jax.experimental import pallas as pl
from jax.experimental.pallas import tpu as pltpu
from jax.sharding import PartitionSpec as P


ITERS = 3
TILE = 128
TILES = 32
SLOTS = 16
SLOT_AT = TILES * SLOTS
CAP = 4
EARLY = 10
REST_AT = 2 * TILES * SLOTS
ZERO = TILES
COLS = 256

carry_weight = 0.9
norm_eps = 1e-05

VMEM = pl.BlockSpec(memory_space=pltpu.VMEM)
SMEM = pl.BlockSpec(memory_space=pltpu.SMEM)
MIB = 1 << 20


def in_vmem(shape, dtype):
    return pltpu.VMEM(shape, dtype)


def tables_kernel(nt_ref, core_ref, table_ref, need_ref, place_ref):
    base = nt_ref[0] - TILES
    direct = jnp.where(core_ref[0] == 0, 2 * TILES, 0)
    swapped = 2 * TILES - direct

    def clear(j, c):
        place_ref[j] = 0
        return c

    lax.fori_loop(0, 3 * TILES, clear, 0)

    def mark(e, c):
        place_ref[nt_ref[e] - base] = 1
        return c

    lax.fori_loop(0, TILES * SLOTS, mark, 0, unroll=8)
    for q in range(128):
        need_ref[q] = 0

    def name(j, c):
        count_direct, count_swapped = c
        is_direct = place_ref[direct + j]
        is_swapped = place_ref[swapped + j]

        @pl.when(is_direct == 1)
        def _():
            need_ref[jnp.minimum(count_direct, CAP - 1)] = j

        place_ref[direct + j] = ZERO + 1 + count_direct
        place_ref[swapped + j] = ZERO + 1 + CAP + count_swapped
        place_ref[j + TILES] = j
        return count_direct + is_direct, count_swapped + is_swapped

    lax.fori_loop(0, TILES, name, (0, 0))

    def row(t, total):
        head, tail = t * SLOTS, t * SLOTS + SLOTS - 1
        for k in range(SLOTS):
            off = nt_ref[t * SLOTS + k] - base
            own = ((off >= TILES) & (off < 2 * TILES)).astype(jnp.int32)
            at = jnp.where(own == 1, head, tail)
            table_ref[at] = place_ref[off]
            table_ref[SLOT_AT + at] = t * SLOTS + k
            head = head + own
            tail = tail - (1 - own)
        rest = jnp.maximum(EARLY - (head - t * SLOTS), 0)
        table_ref[REST_AT + t] = rest
        return total + rest

    table_ref[REST_AT + TILES] = lax.fori_loop(0, TILES, row, 0)


def tables(nt, core):
    i32 = lambda k: jax.ShapeDtypeStruct((k,), jnp.int32)
    return pl.pallas_call(
        tables_kernel,
        out_shape=(i32(REST_AT + 128), i32(128)),
        in_specs=[SMEM] * 2,
        out_specs=(SMEM,) * 2,
        scratch_shapes=[pltpu.SMEM((3 * TILES,), jnp.int32)],
        compiler_params=pltpu.CompilerParams(vmem_limit_bytes=MIB),
        cost_estimate=pl.CostEstimate(flops=0, bytes_accessed=16 * MIB, transcendentals=0),
        name="tables",
    )(nt, core)


def stage_kernel(a_ref, clamp_ref, inv_ref, held_ref, v_ref, sem):
    step = 4
    copies = [
        pltpu.make_async_copy(a_ref.at[pl.ds(g * step, step)], v_ref.at[pl.ds(g * step, step)], sem.at[g])
        for g in range(TILES // step)
    ]
    for c in copies:
        c.start()
    lane = lax.broadcasted_iota(jnp.int32, (TILE, TILE), 1)
    inv_ref[...] = jnp.zeros((TILE, TILE), jnp.float32)
    clamp = clamp_ref[...].astype(jnp.float32)
    held_ref[...] = jnp.concatenate([clamp, jnp.zeros((TILE - TILES, TILE), jnp.float32)], axis=0).T
    for g, c in enumerate(copies):
        c.wait()

        def body(u, carry, g=g):
            t = g * step + u
            total = jnp.zeros((TILE, TILE), jnp.float32)
            for k in range(SLOTS):
                total = total + v_ref[t, k].astype(jnp.float32)
            inv = carry_weight / jnp.sum(total, axis=1, keepdims=True)
            inv_ref[...] = jnp.where(lane == t, inv, inv_ref[...])
            return carry

        lax.fori_loop(0, step, body, 0)


def stage(affinity, clamp):
    return pl.pallas_call(
        stage_kernel,
        out_shape=(
            jax.ShapeDtypeStruct((TILE, TILE), jnp.float32),
            jax.ShapeDtypeStruct((TILE, TILE), jnp.float32),
        ),
        in_specs=[pl.BlockSpec(memory_space=pltpu.HBM), VMEM],
        out_specs=(VMEM,) * 2,
        scratch_shapes=[pltpu.VMEM(affinity.shape, jnp.bfloat16), pltpu.SemaphoreType.DMA((TILES // 4,))],
        compiler_params=pltpu.CompilerParams(vmem_limit_bytes=42 * MIB),
        cost_estimate=pl.CostEstimate(flops=TILES * SLOTS * TILE * TILE, bytes_accessed=16 * MIB, transcendentals=0),
        name="stage",
    )(affinity, clamp)


HALF = (TILES + 1, TILE, TILE)
SEND = (CAP, TILE, COLS)


def order_kernel(order_ref, own_ref, half_ref, src, dst):
    src[...] = own_ref[...].astype(jnp.float32)
    unroll = 64

    def step(i, c):
        base = pl.multiple_of(i * unroll, unroll)
        for u in range(unroll):
            dst[pl.ds(base + u, 1), :] = src[pl.ds(order_ref[base + u], 1), :]
        return c

    lax.fori_loop(0, TILES * TILE // unroll, step, 0)
    half_ref[0:TILES] = dst[...].astype(jnp.bfloat16).reshape(TILES, TILE, TILE)
    half_ref[ZERO] = jnp.zeros((TILE, TILE), jnp.bfloat16)


def order_rows(order, own):
    return pl.pallas_call(
        order_kernel,
        out_shape=in_vmem(HALF, jnp.bfloat16),
        in_specs=[SMEM, VMEM],
        out_specs=VMEM,
        scratch_shapes=[pltpu.VMEM((TILES * TILE, TILE), jnp.float32)] * 2,
        compiler_params=pltpu.CompilerParams(vmem_limit_bytes=8 * MIB),
        cost_estimate=pl.CostEstimate(flops=0, bytes_accessed=32 * MIB, transcendentals=0),
        name="order_rows",
    )(order, own)


def labels_of(refs, tile):
    parts = [ref[tile] for ref in refs]
    return parts[0] if len(parts) == 1 else jnp.concatenate(parts, axis=1)


def pack_kernel(asked, *refs):
    for r in range(CAP):
        refs[-1][r] = labels_of(refs[:-1], asked[r])


def pack(asked, labels):
    return pl.pallas_call(
        pack_kernel,
        out_shape=in_vmem(SEND, jnp.bfloat16),
        in_specs=[SMEM] + [VMEM] * len(labels),
        out_specs=VMEM,
        compiler_params=pltpu.CompilerParams(vmem_limit_bytes=MIB),
        name="pack",
    )(asked, *labels)


def early_kernel(load, table, a_ref, *refs):
    unroll = 4
    if load:
        labels, (acc_ref, v_ref, sem) = refs[:-3], refs[-3:]
    else:
        labels, acc_ref, v_ref = refs[:-1], refs[-1], a_ref

    def copy(g):
        part = pl.ds(g * unroll * SLOTS, unroll * SLOTS)
        return pltpu.make_async_copy(a_ref.at[part], v_ref.at[part], sem.at[g])

    if load:
        for g in range(TILES // unroll):
            copy(g).start()

    def step(g, c):
        if load:
            copy(g).wait()
        for u in range(unroll):
            t = g * unroll + u
            lhs, rhs = [], []
            for k in range(EARLY):
                lhs.append(v_ref[table[SLOT_AT + t * SLOTS + k]])
                rhs.append(labels_of(labels, jnp.minimum(table[t * SLOTS + k], ZERO)))
            acc_ref[t] = jnp.dot(
                jnp.concatenate(lhs, axis=1), jnp.concatenate(rhs, axis=0), preferred_element_type=jnp.float32
            )
        return c

    lax.fori_loop(0, TILES // unroll, step, 0)


def early(table, a, labels, load=False):
    flops = 2 * TILES * EARLY * TILE * TILE * COLS
    acc = in_vmem((TILES, TILE, COLS), jnp.float32)
    return pl.pallas_call(
        functools.partial(early_kernel, load),
        out_shape=(acc, in_vmem(a.shape, a.dtype)) if load else acc,
        in_specs=[SMEM, pl.BlockSpec(memory_space=pltpu.HBM) if load else VMEM] + [VMEM] * len(labels),
        out_specs=(VMEM, VMEM) if load else VMEM,
        scratch_shapes=[pltpu.SemaphoreType.DMA((TILES // 4,))] if load else [],
        compiler_params=pltpu.CompilerParams(vmem_limit_bytes=(28 if load else 8) * MIB),
        cost_estimate=pl.CostEstimate(flops=flops, bytes_accessed=16 * MIB, transcendentals=0),
        name="early_load" if load else "early",
    )(table, a, *labels)


def gather_pool(every, labels, direct_ref, swapped_ref):
    if len(labels) > 1:
        for p, ref in enumerate(labels):
            every[0 : TILES + 1, :, p * TILE : (p + 1) * TILE] = ref[...]
    every[TILES + 1 : TILES + 1 + CAP] = direct_ref[...]
    every[TILES + 1 + CAP :, :, :TILE] = swapped_ref[:, :, TILE:]
    every[TILES + 1 + CAP :, :, TILE:] = swapped_ref[:, :, :TILE]


def add_rest(table, a_ref, every, acc_ref):
    @pl.when(table[REST_AT + TILES] > 0)
    def _():
        def row(t, c):
            def one(r, c):
                at = t * SLOTS + EARLY - 1 - r
                acc_ref[t] = acc_ref[t] + jnp.dot(
                    a_ref[table[SLOT_AT + at]], every[table[at]], preferred_element_type=jnp.float32
                )
                return c

            return lax.fori_loop(0, table[REST_AT + t], one, c)

        lax.fori_loop(0, TILES, row, 0)


def new_labels(table, a_ref, every, acc_ref, inv_ref, held_ref, seeds, t, width):
    lhs, rhs = [], []
    for k in range(EARLY, SLOTS):
        lhs.append(a_ref[table[SLOT_AT + t * SLOTS + k]])
        rhs.append(every[table[t * SLOTS + k]])
    spread = acc_ref[t] + jnp.dot(
        jnp.concatenate(lhs, axis=1), jnp.concatenate(rhs, axis=0), preferred_element_type=jnp.float32
    )
    mine = lax.broadcasted_iota(jnp.int32, (TILE, TILE), 1) == t
    inv = jnp.sum(jnp.where(mine, inv_ref[...], 0.0), axis=1, keepdims=True)
    held = jnp.sum(jnp.where(mine, held_ref[...], 0.0), axis=1, keepdims=True)
    seed = jnp.concatenate([ref[t] for ref in seeds], axis=1).astype(jnp.float32)
    mixed = spread * inv + (1.0 - carry_weight) * seed
    square = mixed * mixed
    mean = jnp.sum(square[:, :TILE] + square[:, TILE:], axis=1, keepdims=True) * (1.0 / COLS)
    scaled = mixed[:, :width] * lax.rsqrt(mean + norm_eps)
    return jnp.where(held > 0.5, seed[:, :width], scaled).astype(jnp.bfloat16)


def asked_kernel(table, asked, a_ref, acc_in, direct_ref, swapped_ref, inv_ref, held_ref, *refs):
    labels, seeds, (acc_ref, every, send_ref) = refs[:-5], refs[-5:-3], refs[-3:]
    gather_pool(every, labels, direct_ref, swapped_ref)
    add_rest(table, a_ref, every, acc_ref)
    for r in range(CAP):
        send_ref[r] = new_labels(table, a_ref, every, acc_ref, inv_ref, held_ref, seeds, asked[r], COLS)


def asked_tiles(table, asked, a, acc, direct, swapped, inv, held, labels, seeds):
    return pl.pallas_call(
        asked_kernel,
        out_shape=(
            in_vmem((TILES, TILE, COLS), jnp.float32),
            in_vmem(EVERY, jnp.bfloat16),
            in_vmem(SEND, jnp.bfloat16),
        ),
        in_specs=[SMEM] * 2 + [VMEM] * (6 + len(labels) + len(seeds)),
        out_specs=(VMEM,) * 3,
        input_output_aliases={3: 0, 8: 1} if len(labels) == 1 else {3: 0},
        compiler_params=pltpu.CompilerParams(vmem_limit_bytes=4 * MIB),
        name="asked_tiles",
    )(table, asked, a, acc, direct, swapped, inv, held, *labels, *seeds)


EVERY = (TILES + 1 + 2 * CAP, TILE, COLS)


def all_kernel(table, a_ref, acc_ref, every, inv_ref, held_ref, *refs):
    seeds, new_ref = refs[:-1], refs[-1]
    unroll = 4

    def step(g, c):
        for u in range(unroll):
            t = g * unroll + u
            new_ref[t] = new_labels(table, a_ref, every, acc_ref, inv_ref, held_ref, seeds, t, COLS)
        return c

    lax.fori_loop(0, TILES // unroll, step, 0)
    new_ref[ZERO] = jnp.zeros((TILE, COLS), jnp.bfloat16)


def all_tiles(table, a, acc, every, inv, held, seeds):
    flops = 2 * TILES * (SLOTS - EARLY) * TILE * TILE * COLS
    return pl.pallas_call(
        all_kernel,
        out_shape=in_vmem(EVERY, jnp.bfloat16),
        in_specs=[SMEM] + [VMEM] * (5 + len(seeds)),
        out_specs=VMEM,
        compiler_params=pltpu.CompilerParams(vmem_limit_bytes=8 * MIB),
        cost_estimate=pl.CostEstimate(flops=flops, bytes_accessed=16 * MIB, transcendentals=0),
        name="all_tiles",
    )(table, a, acc, every, inv, held, *seeds)


def last_kernel(table, a_ref, acc_in, direct_ref, swapped_ref, inv_ref, held_ref, *refs):
    labels, seeds, (acc_ref, every, out_ref) = refs[:-5], refs[-5:-3], refs[-3:]
    gather_pool(every, labels, direct_ref, swapped_ref)
    add_rest(table, a_ref, every, acc_ref)
    unroll = 4

    def step(g, c):
        for u in range(unroll):
            t = g * unroll + u
            out_ref[t] = new_labels(table, a_ref, every, acc_ref, inv_ref, held_ref, seeds, t, TILE)
        return c

    lax.fori_loop(0, TILES // unroll, step, 0)


def last_tiles(table, a, acc, direct, swapped, inv, held, labels, seeds):
    return pl.pallas_call(
        last_kernel,
        out_shape=(
            in_vmem((TILES, TILE, COLS), jnp.float32),
            in_vmem(EVERY, jnp.bfloat16),
            jax.ShapeDtypeStruct((TILES, TILE, TILE), jnp.bfloat16),
        ),
        in_specs=[SMEM] + [VMEM] * (6 + len(labels) + len(seeds)),
        out_specs=(VMEM,) * 3,
        input_output_aliases={2: 0, 7: 1},
        compiler_params=pltpu.CompilerParams(vmem_limit_bytes=8 * MIB),
        name="last_tiles",
    )(table, a, acc, direct, swapped, inv, held, *labels, *seeds)[2]


def shifted(block, step):
    parts, cores = lax.axis_size("dom"), lax.axis_size("col")
    route = []
    for i in range(parts):
        for core, to in ((0, i + step), (1, i - step)):
            if 0 <= to < parts:
                route.append((i * cores + core, to * cores + core))
    return lax.ppermute(block, ("dom", "col"), route)


def swapped_cores(block):
    return lax.ppermute(block, "col", [(0, 1), (1, 0)])


def per_device(seed_data, dataset_order, affinity, neighbour_tiles, clamp_mask):
    part_count = lax.axis_size("dom")
    cell_count, slab = seed_data.shape
    pieces = seed_data.reshape(part_count, cell_count // part_count, slab)
    own = lax.all_to_all(pieces, "dom", split_axis=0, concat_axis=0, tiled=True).reshape(cell_count, slab)
    core = lax.axis_index("col").astype(jnp.int32).reshape(1)
    table, need = tables(neighbour_tiles.reshape(-1), core)
    asked = shifted(need, 1)
    inv, held = stage(affinity, clamp_mask.reshape(TILES, TILE))
    a = affinity.reshape(TILES * SLOTS, TILE, TILE)
    half = order_rows(dataset_order.reshape(-1), own)
    labels = (half, swapped_cores(half))
    seeds = labels
    send = pack(asked, labels)
    for iteration in range(ITERS):
        direct = shifted(send, -1)
        if iteration > 0:
            labels = (all_tiles(table, a, acc, every, inv, held, seeds),)
        if iteration:
            acc = early(table, a, labels)
        else:
            acc, a = early(table, a, labels, load=True)
        swapped = swapped_cores(direct)
        if iteration == ITERS - 1:
            result = last_tiles(table, a, acc, direct, swapped, inv, held, labels, seeds)
            return result.reshape(cell_count, slab)
        acc, every, send = asked_tiles(table, asked, a, acc, direct, swapped, inv, held, labels, seeds)


def solution(mesh):
    return jax.shard_map(
        per_device,
        mesh=mesh,
        in_specs=(
            P("dom", "col"),
            P("dom", None),
            P("dom", None, None, None),
            P("dom", None),
            P("dom"),
        ),
        out_specs=P("dom", "col"),
        check_vma=False,
    )
```

```python
import functools

import jax
import jax.numpy as jnp
from jax import lax
from jax.experimental import pallas as pl
from jax.experimental.pallas import tpu as pltpu
from jax.sharding import PartitionSpec as P


ITERS = 3
TILE = 128
TILES = 32
SLOTS = 16
SLOT_AT = TILES * SLOTS
CAP = 4
EARLY = 10
REST_AT = 2 * TILES * SLOTS
ZERO = TILES
COLS = 256

carry_weight = 0.9
norm_eps = 1e-05

VMEM = pl.BlockSpec(memory_space=pltpu.VMEM)
SMEM = pl.BlockSpec(memory_space=pltpu.SMEM)
MIB = 1 << 20


def in_vmem(shape, dtype):
    return pltpu.VMEM(shape, dtype)


def tables_kernel(nt_ref, core_ref, table_ref, need_ref, place_ref):
    base = nt_ref[0] - TILES
    direct = jnp.where(core_ref[0] == 0, 2 * TILES, 0)
    swapped = 2 * TILES - direct

    def clear(j, c):
        place_ref[j] = 0
        return c

    lax.fori_loop(0, 3 * TILES, clear, 0)

    def mark(e, c):
        place_ref[nt_ref[e] - base] = 1
        return c

    lax.fori_loop(0, TILES * SLOTS, mark, 0, unroll=8)
    for q in range(128):
        need_ref[q] = 0

    def name(j, c):
        count_direct, count_swapped = c
        is_direct = place_ref[direct + j]
        is_swapped = place_ref[swapped + j]

        @pl.when(is_direct == 1)
        def _():
            need_ref[jnp.minimum(count_direct, CAP - 1)] = j

        place_ref[direct + j] = ZERO + 1 + count_direct
        place_ref[swapped + j] = ZERO + 1 + CAP + count_swapped
        place_ref[j + TILES] = j
        return count_direct + is_direct, count_swapped + is_swapped

    lax.fori_loop(0, TILES, name, (0, 0))

    def row(t, total):
        head, tail = t * SLOTS, t * SLOTS + SLOTS - 1
        for k in range(SLOTS):
            off = nt_ref[t * SLOTS + k] - base
            own = ((off >= TILES) & (off < 2 * TILES)).astype(jnp.int32)
            at = jnp.where(own == 1, head, tail)
            table_ref[at] = place_ref[off]
            table_ref[SLOT_AT + at] = t * SLOTS + k
            head = head + own
            tail = tail - (1 - own)
        rest = jnp.maximum(EARLY - (head - t * SLOTS), 0)
        table_ref[REST_AT + t] = rest
        return total + rest

    table_ref[REST_AT + TILES] = lax.fori_loop(0, TILES, row, 0)


def tables(nt, core):
    i32 = lambda k: jax.ShapeDtypeStruct((k,), jnp.int32)
    return pl.pallas_call(
        tables_kernel,
        out_shape=(i32(REST_AT + 128), i32(128)),
        in_specs=[SMEM] * 2,
        out_specs=(SMEM,) * 2,
        scratch_shapes=[pltpu.SMEM((3 * TILES,), jnp.int32)],
        compiler_params=pltpu.CompilerParams(vmem_limit_bytes=MIB),
        cost_estimate=pl.CostEstimate(flops=0, bytes_accessed=16 * MIB, transcendentals=0),
        name="tables",
    )(nt, core)


def stage_kernel(a_ref, clamp_ref, inv_ref, v_ref, sem):
    step = 4
    copies = [
        pltpu.make_async_copy(a_ref.at[pl.ds(g * step, step)], v_ref.at[pl.ds(g * step, step)], sem.at[g])
        for g in range(TILES // step)
    ]
    for c in copies:
        c.start()
    lane = lax.broadcasted_iota(jnp.int32, (TILE, TILE), 1)
    inv_ref[...] = jnp.zeros((TILE, TILE), jnp.float32)
    clamp = clamp_ref[...].astype(jnp.float32)
    held = jnp.concatenate([clamp, jnp.zeros((TILE - TILES, TILE), jnp.float32)], axis=0).T > 0.5
    for g, c in enumerate(copies):
        c.wait()

        def body(u, carry, g=g):
            t = g * step + u
            total = jnp.zeros((TILE, TILE), jnp.float32)
            for k in range(SLOTS):
                total = total + v_ref[t, k].astype(jnp.float32)
            inv = carry_weight / jnp.sum(total, axis=1, keepdims=True)
            inv_ref[...] = jnp.where(lane == t, inv, inv_ref[...])
            return carry

        lax.fori_loop(0, step, body, 0)
    inv_ref[...] = jnp.where(held, -inv_ref[...], inv_ref[...])


def stage(affinity, clamp):
    return pl.pallas_call(
        stage_kernel,
        out_shape=jax.ShapeDtypeStruct((TILE, TILE), jnp.float32),
        in_specs=[pl.BlockSpec(memory_space=pltpu.HBM), VMEM],
        out_specs=VMEM,
        scratch_shapes=[pltpu.VMEM(affinity.shape, jnp.bfloat16), pltpu.SemaphoreType.DMA((TILES // 4,))],
        compiler_params=pltpu.CompilerParams(vmem_limit_bytes=42 * MIB),
        cost_estimate=pl.CostEstimate(flops=TILES * SLOTS * TILE * TILE, bytes_accessed=16 * MIB, transcendentals=0),
        name="stage",
    )(affinity, clamp)


HALF = (TILES + 1, TILE, TILE)
SEND = (CAP, TILE, COLS)


def order_kernel(order_ref, own_ref, half_ref, src, dst):
    src[...] = own_ref[...].astype(jnp.float32)
    unroll = 64

    def step(i, c):
        base = pl.multiple_of(i * unroll, unroll)
        for u in range(unroll):
            dst[pl.ds(base + u, 1), :] = src[pl.ds(order_ref[base + u], 1), :]
        return c

    lax.fori_loop(0, TILES * TILE // unroll, step, 0)
    half_ref[0:TILES] = dst[...].astype(jnp.bfloat16).reshape(TILES, TILE, TILE)
    half_ref[ZERO] = jnp.zeros((TILE, TILE), jnp.bfloat16)


def order_rows(order, own):
    return pl.pallas_call(
        order_kernel,
        out_shape=in_vmem(HALF, jnp.bfloat16),
        in_specs=[SMEM, VMEM],
        out_specs=VMEM,
        scratch_shapes=[pltpu.VMEM((TILES * TILE, TILE), jnp.float32)] * 2,
        compiler_params=pltpu.CompilerParams(vmem_limit_bytes=8 * MIB),
        cost_estimate=pl.CostEstimate(flops=0, bytes_accessed=32 * MIB, transcendentals=0),
        name="order_rows",
    )(order, own)


def labels_of(refs, tile):
    parts = [ref[tile] for ref in refs]
    return parts[0] if len(parts) == 1 else jnp.concatenate(parts, axis=1)


def pack_kernel(asked, *refs):
    for r in range(CAP):
        refs[-1][r] = labels_of(refs[:-1], asked[r])


def pack(asked, labels):
    return pl.pallas_call(
        pack_kernel,
        out_shape=in_vmem(SEND, jnp.bfloat16),
        in_specs=[SMEM] + [VMEM] * len(labels),
        out_specs=VMEM,
        compiler_params=pltpu.CompilerParams(vmem_limit_bytes=MIB),
        name="pack",
    )(asked, *labels)


def early_kernel(load, table, a_ref, *refs):
    unroll = 4
    if load:
        labels, (acc_ref, v_ref, sem) = refs[:-3], refs[-3:]
    else:
        labels, acc_ref, v_ref = refs[:-1], refs[-1], a_ref

    def copy(g):
        part = pl.ds(g * unroll * SLOTS, unroll * SLOTS)
        return pltpu.make_async_copy(a_ref.at[part], v_ref.at[part], sem.at[g])

    if load:
        for g in range(TILES // unroll):
            copy(g).start()

    def step(g, c):
        if load:
            copy(g).wait()
        for u in range(unroll):
            t = g * unroll + u
            lhs, rhs = [], []
            for k in range(EARLY):
                lhs.append(v_ref[table[SLOT_AT + t * SLOTS + k]])
                rhs.append(labels_of(labels, jnp.minimum(table[t * SLOTS + k], ZERO)))
            acc_ref[t] = jnp.dot(
                jnp.concatenate(lhs, axis=1), jnp.concatenate(rhs, axis=0), preferred_element_type=jnp.float32
            )
        return c

    lax.fori_loop(0, TILES // unroll, step, 0)


def early(table, a, labels, load=False):
    flops = 2 * TILES * EARLY * TILE * TILE * COLS
    acc = in_vmem((TILES, TILE, COLS), jnp.float32)
    return pl.pallas_call(
        functools.partial(early_kernel, load),
        out_shape=(acc, in_vmem(a.shape, a.dtype)) if load else acc,
        in_specs=[SMEM, pl.BlockSpec(memory_space=pltpu.HBM) if load else VMEM] + [VMEM] * len(labels),
        out_specs=(VMEM, VMEM) if load else VMEM,
        scratch_shapes=[pltpu.SemaphoreType.DMA((TILES // 4,))] if load else [],
        compiler_params=pltpu.CompilerParams(vmem_limit_bytes=(28 if load else 8) * MIB),
        cost_estimate=pl.CostEstimate(flops=flops, bytes_accessed=16 * MIB, transcendentals=0),
        name="early_load" if load else "early",
    )(table, a, *labels)


def gather_pool(every, labels, direct_ref, swapped_ref):
    if len(labels) > 1:
        for p, ref in enumerate(labels):
            every[0 : TILES + 1, :, p * TILE : (p + 1) * TILE] = ref[...]
    every[TILES + 1 : TILES + 1 + CAP] = direct_ref[...]
    every[TILES + 1 + CAP :, :, :TILE] = swapped_ref[:, :, TILE:]
    every[TILES + 1 + CAP :, :, TILE:] = swapped_ref[:, :, :TILE]


def add_rest(table, a_ref, every, acc_ref):
    @pl.when(table[REST_AT + TILES] > 0)
    def _():
        def row(t, c):
            def one(r, c):
                at = t * SLOTS + EARLY - 1 - r
                acc_ref[t] = acc_ref[t] + jnp.dot(
                    a_ref[table[SLOT_AT + at]], every[table[at]], preferred_element_type=jnp.float32
                )
                return c

            return lax.fori_loop(0, table[REST_AT + t], one, c)

        lax.fori_loop(0, TILES, row, 0)


def new_labels(table, a_ref, every, acc_ref, inv_ref, seeds, t, width):
    lhs, rhs = [], []
    for k in range(EARLY, SLOTS):
        lhs.append(a_ref[table[SLOT_AT + t * SLOTS + k]])
        rhs.append(every[table[t * SLOTS + k]])
    spread = acc_ref[t] + jnp.dot(
        jnp.concatenate(lhs, axis=1), jnp.concatenate(rhs, axis=0), preferred_element_type=jnp.float32
    )
    mine = lax.broadcasted_iota(jnp.int32, (TILE, TILE), 1) == t
    inv = jnp.sum(jnp.where(mine, inv_ref[...], 0.0), axis=1, keepdims=True)
    seed = jnp.concatenate([ref[t] for ref in seeds], axis=1).astype(jnp.float32)
    mixed = spread * inv + (1.0 - carry_weight) * seed
    square = mixed * mixed
    mean = jnp.sum(square[:, :TILE] + square[:, TILE:], axis=1, keepdims=True) * (1.0 / COLS)
    scaled = mixed[:, :width] * lax.rsqrt(mean + norm_eps)
    return jnp.where(inv < 0.0, seed[:, :width], scaled).astype(jnp.bfloat16)


def asked_kernel(table, asked, a_ref, acc_in, direct_ref, swapped_ref, inv_ref, *refs):
    labels, seeds, (acc_ref, every, send_ref) = refs[:-5], refs[-5:-3], refs[-3:]
    gather_pool(every, labels, direct_ref, swapped_ref)
    add_rest(table, a_ref, every, acc_ref)
    for r in range(CAP):
        send_ref[r] = new_labels(table, a_ref, every, acc_ref, inv_ref, seeds, asked[r], COLS)


def asked_tiles(table, asked, a, acc, direct, swapped, inv, labels, seeds):
    return pl.pallas_call(
        asked_kernel,
        out_shape=(
            in_vmem((TILES, TILE, COLS), jnp.float32),
            in_vmem(EVERY, jnp.bfloat16),
            in_vmem(SEND, jnp.bfloat16),
        ),
        in_specs=[SMEM] * 2 + [VMEM] * (5 + len(labels) + len(seeds)),
        out_specs=(VMEM,) * 3,
        input_output_aliases={3: 0, 7: 1} if len(labels) == 1 else {3: 0},
        compiler_params=pltpu.CompilerParams(vmem_limit_bytes=4 * MIB),
        name="asked_tiles",
    )(table, asked, a, acc, direct, swapped, inv, *labels, *seeds)


EVERY = (TILES + 1 + 2 * CAP, TILE, COLS)


def all_kernel(table, a_ref, acc_ref, every, inv_ref, *refs):
    seeds, new_ref = refs[:-1], refs[-1]
    unroll = 8

    def step(g, c):
        for u in range(unroll):
            t = g * unroll + u
            new_ref[t] = new_labels(table, a_ref, every, acc_ref, inv_ref, seeds, t, COLS)
        return c

    lax.fori_loop(0, TILES // unroll, step, 0)
    new_ref[ZERO] = jnp.zeros((TILE, COLS), jnp.bfloat16)


def all_tiles(table, a, acc, every, inv, seeds):
    flops = 2 * TILES * (SLOTS - EARLY) * TILE * TILE * COLS
    return pl.pallas_call(
        all_kernel,
        out_shape=in_vmem(EVERY, jnp.bfloat16),
        in_specs=[SMEM] + [VMEM] * (4 + len(seeds)),
        out_specs=VMEM,
        compiler_params=pltpu.CompilerParams(vmem_limit_bytes=8 * MIB),
        cost_estimate=pl.CostEstimate(flops=flops, bytes_accessed=16 * MIB, transcendentals=0),
        name="all_tiles",
    )(table, a, acc, every, inv, *seeds)


def last_kernel(table, a_ref, acc_in, direct_ref, swapped_ref, inv_ref, *refs):
    labels, seeds, (acc_ref, every, out_ref) = refs[:-5], refs[-5:-3], refs[-3:]
    gather_pool(every, labels, direct_ref, swapped_ref)
    add_rest(table, a_ref, every, acc_ref)
    unroll = 8

    def step(g, c):
        for u in range(unroll):
            t = g * unroll + u
            out_ref[t] = new_labels(table, a_ref, every, acc_ref, inv_ref, seeds, t, TILE)
        return c

    lax.fori_loop(0, TILES // unroll, step, 0)


def last_tiles(table, a, acc, direct, swapped, inv, labels, seeds):
    return pl.pallas_call(
        last_kernel,
        out_shape=(
            in_vmem((TILES, TILE, COLS), jnp.float32),
            in_vmem(EVERY, jnp.bfloat16),
            jax.ShapeDtypeStruct((TILES, TILE, TILE), jnp.bfloat16),
        ),
        in_specs=[SMEM] + [VMEM] * (5 + len(labels) + len(seeds)),
        out_specs=(VMEM,) * 3,
        input_output_aliases={2: 0, 6: 1},
        compiler_params=pltpu.CompilerParams(vmem_limit_bytes=8 * MIB),
        name="last_tiles",
    )(table, a, acc, direct, swapped, inv, *labels, *seeds)[2]


def shifted(block, step):
    parts, cores = lax.axis_size("dom"), lax.axis_size("col")
    route = []
    for i in range(parts):
        for core, to in ((0, i + step), (1, i - step)):
            if 0 <= to < parts:
                route.append((i * cores + core, to * cores + core))
    return lax.ppermute(block, ("dom", "col"), route)


def swapped_cores(block):
    return lax.ppermute(block, "col", [(0, 1), (1, 0)])


def per_device(seed_data, dataset_order, affinity, neighbour_tiles, clamp_mask):
    part_count = lax.axis_size("dom")
    cell_count, slab = seed_data.shape
    pieces = seed_data.reshape(part_count, cell_count // part_count, slab)
    own = lax.all_to_all(pieces, "dom", split_axis=0, concat_axis=0, tiled=True).reshape(cell_count, slab)
    core = lax.axis_index("col").astype(jnp.int32).reshape(1)
    table, need = tables(neighbour_tiles.reshape(-1), core)
    asked = shifted(need, 1)
    inv = stage(affinity, clamp_mask.reshape(TILES, TILE))
    a = affinity.reshape(TILES * SLOTS, TILE, TILE)
    half = order_rows(dataset_order.reshape(-1), own)
    labels = (half, swapped_cores(half))
    seeds = labels
    send = pack(asked, labels)
    for iteration in range(ITERS):
        direct = shifted(send, -1)
        if iteration > 0:
            labels = (all_tiles(table, a, acc, every, inv, seeds),)
        if iteration:
            acc = early(table, a, labels)
        else:
            acc, a = early(table, a, labels, load=True)
        swapped = swapped_cores(direct)
        if iteration == ITERS - 1:
            result = last_tiles(table, a, acc, direct, swapped, inv, labels, seeds)
            return result.reshape(cell_count, slab)
        acc, every, send = asked_tiles(table, asked, a, acc, direct, swapped, inv, labels, seeds)


def solution(mesh):
    return jax.shard_map(
        per_device,
        mesh=mesh,
        in_specs=(
            P("dom", "col"),
            P("dom", None),
            P("dom", None, None, None),
            P("dom", None),
            P("dom"),
        ),
        out_specs=P("dom", "col"),
        check_vma=False,
    )
```
